32 devices in a mesh: dp: 8 (over z, core), row: 2 (over x), col: 2 (over y).
Axes of the slice: x: 2, y: 2, z: 4, core: 2. Of those that a mesh axis runs over, the one named last changes fastest.
Arguments:
- tokens: bfloat16 [2, 16384, 768], P(None, ('dp', 'col'), 'row'), may hold values from -6 to 6
- joint_weight: bfloat16 [768, 3, 768], P('row', None, 'col'), may hold values from -0.3125 to 0.3125
- joint_bias: float32 [2, 768], P(None, 'col'), may hold values from -1.75 to 1.75
- out_weight: bfloat16 [768, 768], P('col', 'row'), may hold values from -1.75 to 1.75
- out_bias: float32 [768], P('row'), may hold values from -1.75 to 1.75
- norm_gain: float32 [768], P('row'), may hold values from 0.5 to 1.5
- norm_shift: float32 [768], P('row'), may hold values from -1.75 to 1.75
- inner_weight: bfloat16 [768, 3072], P('row', 'col'), may hold values from -0.21875 to 0.21875
- inner_bias: float32 [3072], P('col'), may hold values from -1.75 to 1.75
- outer_weight: bfloat16 [3072, 768], P('col', 'row'), may hold values from -0.21875 to 0.21875
- outer_bias: float32 [768], P('row'), may hold values from -1.75 to 1.75
- final_gain: float32 [768], P('row'), may hold values from 0.5 to 1.5
- final_shift: float32 [768], P('row'), may hold values from -1.75 to 1.75
- trained_gate_scores: float32 [12, 512, 512], P('col'), may hold values from -6 to 6
- mask_noise: float32 [12, 512, 512], P('col'), may hold values from 0.02 to 0.98
- cotangent: bfloat16 [2, 16384, 768], P(None, ('dp', 'col'), 'row'), may hold values from -6 to 6
Outputs:
- output: bfloat16 [2, 16384, 768], P(None, ('dp', 'col'), 'row')
- grad_tokens: float32 [2, 16384, 768], P(None, ('dp', 'col'), 'row')
- grad_joint_weight: float32 [768, 3, 768], P('row', None, 'col')
- grad_joint_bias: float32 [2, 768], P(None, 'col')
- grad_out_weight: float32 [768, 768], P('col', 'row')
- grad_out_bias: float32 [768], P('row')
- grad_norm_gain: float32 [768], P('row')
- grad_norm_shift: float32 [768], P('row')
- grad_inner_weight: float32 [768, 3072], P('row', 'col')
- grad_inner_bias: float32 [3072], P('col')
- grad_outer_weight: float32 [3072, 768], P('col', 'row')
- grad_outer_bias: float32 [768], P('row')
- grad_final_gain: float32 [768], P('row')
- grad_final_shift: float32 [768], P('row')
- grad_mask_logit: float32 [12, 512, 512], P('col', ('dp', 'row'))
The draws below stay inside these ranges and needn't reach their ends.
All inputs are finite; a program needn't handle non-finite values.
Results may differ from the reference program's by a relative error of at most 0.02.
Values may be sent and summed in bfloat16 or wider, within the bound.
No kernel may reach another device: no remote copies, remote signals or barrier semaphores. Data moves between devices by JAX's collectives and lax.ppermute only.
A program may use at most 896 MiB of HBM per device.

```python
import jax
import jax.numpy as jnp
from jax import lax

D = 768
HEADS = 12
HDIM = 64
FF = 3072
MASK_LEN = 512
PROMPT = 1024
CONT_LEN = 512
MICRO = 2
TGROUP = 2048
SEQ_ALL = 16384
N_DP = 8


def block_scale(stream_key, dims, cuts, low, high):
    loudness, own = 1.0, jax.random.fold_in(stream_key, 6)
    for axis_at, blocks in cuts:
        draws = jnp.exp(jax.random.uniform(jax.random.fold_in(own, axis_at), (blocks,), jnp.float32, low / len(cuts), high / len(cuts)))
        loudness = loudness * jnp.repeat(draws, dims[axis_at] // blocks).reshape([-1 if axis == axis_at else 1 for axis in range(len(dims))])
    return loudness


def centred(stream_key, extent, deviation, most, cuts=(), kind=jnp.bfloat16):
    values = deviation * jax.random.normal(stream_key, extent, jnp.float32)
    if cuts:
        values = values * block_scale(stream_key, extent, cuts, -0.22, 0.18)
    return jnp.clip(values, -most, most).astype(kind)


def setup_inputs(seed: int = 0) -> dict:
    keys = jax.random.split(jax.random.key(seed), 17)
    return {
        "tokens": centred(keys[0], (MICRO, SEQ_ALL, D), 1.0, 6.0, ((1, 16), (2, 2))),
        "joint_weight": centred(keys[1], (D, 3, D), (D // 2) ** -0.5, 0.3125, ((0, 2), (2, 2))),
        "joint_bias": centred(keys[2], (2, D), 0.3, 1.75, ((1, 2),), jnp.float32),
        "out_weight": centred(keys[3], (D, D), (max(D // 64, 1)) ** -0.5, 1.75, ((0, 2), (1, 2))),
        "out_bias": centred(keys[4], (D,), 0.3, 1.75, ((0, 2),), jnp.float32),
        "norm_gain": jnp.clip(1.0 + 0.1 * jax.random.normal(keys[5], (D,), jnp.float32), 0.5, 1.5),
        "norm_shift": centred(keys[6], (D,), 0.3, 1.75, ((0, 2),), jnp.float32),
        "inner_weight": centred(keys[7], (D, FF), D ** -0.5, 0.21875, ((0, 2), (1, 2))),
        "inner_bias": centred(keys[8], (FF,), 0.3, 1.75, ((0, 2),), jnp.float32),
        "outer_weight": centred(keys[9], (FF, D), (FF // 4) ** -0.5, 0.21875, ((0, 2), (1, 2))),
        "outer_bias": centred(keys[10], (D,), 0.3, 1.75, ((0, 2),), jnp.float32),
        "final_gain": jnp.clip(1.0 + 0.1 * jax.random.normal(keys[11], (D,), jnp.float32), 0.5, 1.5),
        "final_shift": centred(keys[12], (D,), 0.3, 1.75, ((0, 2),), jnp.float32),
        "trained_gate_scores": centred(keys[13], (HEADS, MASK_LEN, MASK_LEN), 1.5, 6.0, ((0, 2),), jnp.float32),
        "mask_noise": jnp.clip(0.02 + 0.96000002 * jax.random.uniform(keys[14], (HEADS, MASK_LEN, MASK_LEN), jnp.float32) ** block_scale(keys[14], (HEADS, MASK_LEN, MASK_LEN), ((0, 2),), -0.2, 0.2), 0.02, 0.98),
        "cotangent": centred(keys[15], (MICRO, SEQ_ALL, D), 1.0, 6.0, ((1, 16), (2, 2))),
    }


@jax.custom_vjp
def low(v):
    return lax.optimization_barrier(v.astype(jnp.bfloat16)).astype(jnp.float32)

@jax.custom_vjp
def low_back(v):
    return v

def low_keep(v):
    return (low(v), None)

def low_pass(kept, grad):
    return (grad,)

def back_keep(v):
    return (v, None)

def back_low(kept, grad):
    return (low(grad),)
low.defvjp(low_keep, low_pass)
low_back.defvjp(back_keep, back_low)
relaxation_heat = 0.75
norm_eps = 1e-12
masked_score = -1e+30

def product(left, right):
    return jnp.dot(left, right, precision=lax.Precision.HIGHEST)

def layer_norm(values, gain, shift):
    center = values - lax.optimization_barrier(jnp.mean(values, axis=-1, keepdims=True))
    spread = lax.optimization_barrier(jnp.mean(center * center, axis=-1, keepdims=True))
    return center * lax.rsqrt(spread + norm_eps) * gain + shift

def visible_table():
    index = jnp.arange(TGROUP, dtype=jnp.int32)
    segment = jnp.where(index < PROMPT, -1, (index - PROMPT) // CONT_LEN)
    same = (segment[:, None] == segment[None, :]) & (index[:, None] >= PROMPT)
    return (index[None, :] < PROMPT) | same

def head_attention(query, keyset, valueset, mask_tile, visible):
    scores = low_back(product(query, keyset.T) * HDIM ** (-0.5))
    scores = jnp.where(visible, scores, masked_score)
    peak = lax.optimization_barrier(jnp.max(scores, axis=-1, keepdims=True))
    expo = jnp.exp(scores - peak)
    weights = low(expo / lax.optimization_barrier(jnp.sum(expo, axis=-1, keepdims=True)) * mask_tile)
    return product(weights, valueset)

def group_forward(params, gate_open_chance, visible, source):
    joint_weight, joint_bias, out_weight, out_bias, norm_gain, norm_shift, inner_weight, inner_bias, outer_weight, outer_bias, final_gain, final_shift = params
    raw = product(source, joint_weight.reshape(D, 3 * D)).reshape(TGROUP, 3, D)
    zero_row = jnp.zeros((D,), jnp.float32)
    raw = raw + jnp.stack([joint_bias[0], zero_row, joint_bias[1]])
    joint = low_back(low(raw))
    query = joint[:, 0].reshape(TGROUP, HEADS, HDIM).transpose(1, 0, 2)
    keyset = joint[:, 1].reshape(TGROUP, HEADS, HDIM).transpose(1, 0, 2)
    valueset = joint[:, 2].reshape(TGROUP, HEADS, HDIM).transpose(1, 0, 2)
    repeats = TGROUP // MASK_LEN

    def per_head(pieces):
        query_head, key_head, value_head, mask_head = pieces
        return head_attention(query_head, key_head, value_head, jnp.tile(mask_head, (repeats, repeats)), visible)
    heads_out = lax.map(jax.checkpoint(per_head), (query, keyset, valueset, gate_open_chance))
    attended = low_back(low(heads_out.transpose(1, 0, 2).reshape(TGROUP, D)))
    branch = low_back(product(attended, out_weight) + out_bias)
    hidden = layer_norm(source + branch, norm_gain, norm_shift)
    inner = low_back(product(low(hidden), inner_weight) + inner_bias)
    active = low(jax.nn.gelu(inner, approximate=False))
    outer = low_back(product(active, outer_weight) + outer_bias)
    return layer_norm(hidden + outer, final_gain, final_shift)

def forward(params, trained_gate_scores, sigmoid_squash, values):
    gate_open_chance = jax.nn.sigmoid((trained_gate_scores + sigmoid_squash) / relaxation_heat)
    visible = visible_table()
    groups = values.reshape(MICRO * N_DP, TGROUP, D)

    def step_group(carry, group):
        return (carry, jax.checkpoint(group_forward)(params, gate_open_chance, visible, group))
    carry, outs = lax.scan(step_group, jnp.zeros((), jnp.float32), groups)
    return outs.reshape(MICRO, N_DP * TGROUP, D)

def reference(tokens, joint_weight, joint_bias, out_weight, out_bias, norm_gain, norm_shift, inner_weight, inner_bias, outer_weight, outer_bias, final_gain, final_shift, trained_gate_scores, mask_noise, cotangent):
    params = (joint_weight.astype(jnp.float32), joint_bias.astype(jnp.float32), out_weight.astype(jnp.float32), out_bias.astype(jnp.float32), norm_gain.astype(jnp.float32), norm_shift.astype(jnp.float32), inner_weight.astype(jnp.float32), inner_bias.astype(jnp.float32), outer_weight.astype(jnp.float32), outer_bias.astype(jnp.float32), final_gain.astype(jnp.float32), final_shift.astype(jnp.float32))
    sigmoid_squash = jnp.log(mask_noise) - jnp.log1p(-mask_noise)

    def whole_layer(param_set, logits, values):
        return forward(param_set, logits, sigmoid_squash, values)
    result, pull = jax.vjp(whole_layer, params, trained_gate_scores.astype(jnp.float32), tokens.astype(jnp.float32))
    grad_params, gate_backward_factor, grad_input = pull(cotangent.astype(jnp.float32))
    return (result.astype(jnp.bfloat16), grad_input, grad_params[0], grad_params[1], grad_params[2], grad_params[3], grad_params[4], grad_params[5], grad_params[6], grad_params[7], grad_params[8], grad_params[9], grad_params[10], grad_params[11], gate_backward_factor)
```

```python
import jax
import jax.numpy as jnp
from jax import lax
from jax.experimental import pallas as pl
from jax.experimental.pallas import tpu as pltpu
from jax.sharding import PartitionSpec as P

D = 768
HDIM = 64
MASK_LEN = 512
PROMPT = 1024
CONT_LEN = 512


relaxation_heat = 0.75
norm_eps = 1e-12
masked_score = -1e30


def gather_cols(local):
    return lax.all_gather(local, "col", axis=0, tiled=True)


def gather_rows(local):
    return lax.all_gather(local, "row", axis=0, tiled=True)


def multiply(block, weight, flipped):
    if flipped:
        return lax.dot_general(
            block, weight, (((1,), (1,)), ((), ())), preferred_element_type=jnp.float32
        )
    return jnp.dot(block, weight, preferred_element_type=jnp.float32)


def sum_over_rows(whole, weight, flipped):

    def partial_rows(first, number):
        return multiply(whole, weight, flipped)

    return lax.psum_scatter(
        partial_rows(jnp.int32(0), whole.shape[0] // lax.axis_size("row") * lax.axis_size("row")),
        "row",
        scatter_dimension=0,
        tiled=True,
    )


def sum_over_cols(whole, weight, flipped):

    def partial_rows(first, number):
        return multiply(whole, weight, flipped)

    return lax.psum_scatter(
        partial_rows(jnp.int32(0), whole.shape[0] // lax.axis_size("col") * lax.axis_size("col")),
        "col",
        scatter_dimension=0,
        tiled=True,
    )


def transpose_product(left, right):
    return lax.dot_general(
        left, right, (((0,), (0,)), ((), ())), preferred_element_type=jnp.float32
    )


def row_totals(first, second):
    return lax.psum((jnp.sum(first, axis=-1), jnp.sum(second, axis=-1)), "row")


def norm_forward(values, gain, shift):
    total, squares = row_totals(values, values * values)
    mean = total / D
    spread = squares / D - mean * mean
    scale = lax.rsqrt(spread + norm_eps)[:, None]
    normed = (values - mean[:, None]) * scale
    return (normed, scale, normed * gain + shift)


def norm_backward(grad_out, normed, scale, gain):
    scaled = grad_out * gain
    total, mixed = row_totals(scaled, scaled * normed)
    return scale * (scaled - total[:, None] / D - normed * mixed[:, None] / D)


def exact_gelu(values):
    return jax.nn.gelu(values, approximate=False)


def window_rows(whole, window_start, window, heads_here):
    joined = jnp.concatenate(
        [whole[:PROMPT], lax.dynamic_slice_in_dim(whole, window_start, window, 0)], 0
    )
    return joined.reshape(PROMPT + window, heads_here, HDIM)


def spread_rows(grad_cat, window_start, group_rows):
    width = grad_cat.shape[1] * grad_cat.shape[2]
    flat = grad_cat.reshape(grad_cat.shape[0], width)
    full = jnp.concatenate([flat[:PROMPT], jnp.zeros((group_rows - PROMPT, width), jnp.float32)], 0)
    window_part = flat[PROMPT:]
    current = lax.dynamic_slice_in_dim(full, window_start, window_part.shape[0], 0)
    return lax.dynamic_update_slice_in_dim(full, current + window_part, window_start, 0)


def score_table(query, keys_cat, visible):
    scores = jnp.einsum(
        "qhd,khd->hqk", query, keys_cat, preferred_element_type=jnp.float32
    ) * HDIM ** (-0.5)
    return jnp.where(visible[None], scores, masked_score)


def attend(query, keys_cat, values_cat, visible, mask_table):
    scores = score_table(query, keys_cat, visible)
    peak = jnp.max(scores, axis=-1, keepdims=True)
    expo = jnp.exp(scores - peak)
    total = jnp.sum(expo, axis=-1, keepdims=True)
    weights = (expo / total * mask_table).astype(jnp.bfloat16)
    mixed = jnp.einsum("hqk,khd->qhd", weights, values_cat, preferred_element_type=jnp.float32)
    return (mixed, peak + jnp.log(total))


def attend_back(query, keys_cat, values_cat, visible, mask_table, log_total, grad_mixed):
    prob = jnp.exp(score_table(query, keys_cat, visible) - log_total)
    weights = (prob * mask_table).astype(jnp.bfloat16)
    value_sensitivity = jnp.einsum(
        "hqk,qhd->khd", weights, grad_mixed, preferred_element_type=jnp.float32
    )
    grad_weights = jnp.einsum(
        "qhd,khd->hqk", grad_mixed, values_cat, preferred_element_type=jnp.float32
    )
    grad_prob = grad_weights * mask_table
    grad_scores = prob * (grad_prob - jnp.sum(grad_prob * prob, axis=-1, keepdims=True))
    grad_low = grad_scores.astype(jnp.bfloat16)
    grad_query = jnp.einsum(
        "hqk,khd->qhd", grad_low, keys_cat, preferred_element_type=jnp.float32
    ) * HDIM ** (-0.5)
    grad_keys = jnp.einsum(
        "hqk,qhd->khd", grad_low, query, preferred_element_type=jnp.float32
    ) * HDIM ** (-0.5)
    return (grad_query, grad_keys, value_sensitivity, grad_weights * prob)


def fold_mask(part, row_offset):
    heads_here, block_rows, width = part.shape
    folded = part.reshape(heads_here, block_rows, width // MASK_LEN, MASK_LEN).sum(2)
    if block_rows >= MASK_LEN:
        return folded.reshape(heads_here, block_rows // MASK_LEN, MASK_LEN, MASK_LEN).sum(1)
    blank = jnp.zeros((heads_here, MASK_LEN, MASK_LEN), jnp.float32)
    return lax.dynamic_update_slice_in_dim(blank, folded, row_offset, 1)


def reduce_params(weight_part, norm_part):
    weight_sum = (
        lax.psum(weight_part[0].astype(jnp.bfloat16), "dp").astype(jnp.float32),
        lax.psum(weight_part[1].astype(jnp.bfloat16), "dp").astype(jnp.float32),
        lax.psum(weight_part[2].astype(jnp.bfloat16), "dp").astype(jnp.float32),
        lax.psum(weight_part[3].astype(jnp.bfloat16), "dp").astype(jnp.float32),
        lax.psum(weight_part[4].astype(jnp.bfloat16), "dp").astype(jnp.float32),
        lax.psum(weight_part[5].astype(jnp.bfloat16), "dp").astype(jnp.float32),
        lax.psum(weight_part[6].astype(jnp.bfloat16), "dp").astype(jnp.float32),
        lax.psum(weight_part[7].astype(jnp.bfloat16), "dp").astype(jnp.float32),
    )
    norm_sum = lax.psum((norm_part[0], norm_part[1], norm_part[2], norm_part[3]), ("dp", "col"))
    return (tuple(weight_sum), tuple(norm_sum))


def collapse_mask_gradient(mask_part):
    return lax.psum_scatter(mask_part, ("dp", "row"), scatter_dimension=1, tiled=True)


def on_device(
    tokens,
    joint_weight,
    joint_bias,
    out_weight,
    out_bias,
    norm_gain,
    norm_shift,
    inner_weight,
    inner_bias,
    outer_weight,
    outer_bias,
    final_gain,
    final_shift,
    trained_gate_scores,
    mask_noise,
    cotangent,
):
    micro, half_rows, row_width = tokens.shape
    heads_here = trained_gate_scores.shape[0]
    col_width = joint_weight.shape[2]
    joint_flat = joint_weight.reshape(row_width, 3 * col_width)
    sigmoid_squash = jnp.log(mask_noise) - jnp.log1p(-mask_noise)
    gate_open_chance = jax.nn.sigmoid((trained_gate_scores + sigmoid_squash) / relaxation_heat)
    group_rows = half_rows * lax.axis_size("col")
    block_rows = group_rows // lax.axis_size("row")
    window = max(block_rows, CONT_LEN)
    start = lax.axis_index("row") * block_rows
    window_start = start - start % window
    row_offset = start % MASK_LEN
    query_pos = start + jnp.arange(block_rows, dtype=jnp.int32)
    key_pos = window_start + jnp.arange(window, dtype=jnp.int32)
    same = (query_pos[:, None] - PROMPT) // CONT_LEN == (key_pos[None, :] - PROMPT) // CONT_LEN
    tail = (query_pos[:, None] >= PROMPT) & (key_pos[None, :] >= PROMPT) & same
    visible = jnp.concatenate([jnp.ones((block_rows, PROMPT), jnp.bool_), tail], 1)
    if block_rows >= MASK_LEN:
        mask_rows = jnp.tile(gate_open_chance, (1, block_rows // MASK_LEN, 1))
    else:
        mask_rows = lax.dynamic_slice_in_dim(gate_open_chance, row_offset, block_rows, 1)
    mask_table = jnp.tile(mask_rows, (1, 1, (PROMPT + window) // MASK_LEN))
    bias_rows = jnp.stack([joint_bias[0], jnp.zeros_like(joint_bias[0]), joint_bias[1]])
    weight_acc = (
        jnp.zeros((row_width, 3 * col_width), jnp.float32),
        jnp.zeros((2, col_width), jnp.float32),
        jnp.zeros(out_weight.shape, jnp.float32),
        jnp.zeros(out_bias.shape, jnp.float32),
        jnp.zeros(inner_weight.shape, jnp.float32),
        jnp.zeros(inner_bias.shape, jnp.float32),
        jnp.zeros(outer_weight.shape, jnp.float32),
        jnp.zeros(outer_bias.shape, jnp.float32),
    )
    norm_acc = (
        jnp.zeros((row_width,), jnp.float32),
        jnp.zeros((row_width,), jnp.float32),
        jnp.zeros((row_width,), jnp.float32),
        jnp.zeros((row_width,), jnp.float32),
    )
    gate_running_total = jnp.zeros(gate_open_chance.shape, jnp.float32)
    outcome_list = []
    grad_list = []
    for micro_index in range(micro):
        source = tokens[micro_index]
        source_all = gather_cols(source)
        joint_raw = (
            sum_over_rows(source_all, joint_flat, False).reshape(block_rows, 3, col_width)
            + bias_rows
        )
        joint_low = joint_raw.astype(jnp.bfloat16)
        keys_all, values_all = (
            lax.all_gather(joint_low[:, 1], "row", axis=0, tiled=True),
            lax.all_gather(joint_low[:, 2], "row", axis=0, tiled=True),
        )
        keys_cat = window_rows(keys_all, window_start, window, heads_here)
        values_cat = window_rows(values_all, window_start, window, heads_here)
        query = joint_low[:, 0].reshape(block_rows, heads_here, HDIM)
        mixed, log_total = attend(query, keys_cat, values_cat, visible, mask_table)
        attended_all = gather_rows(mixed.reshape(block_rows, col_width).astype(jnp.bfloat16))
        branch = sum_over_cols(attended_all, out_weight, False) + out_bias
        normed_one, scale_one, hidden = norm_forward(
            source.astype(jnp.float32) + branch, norm_gain, norm_shift
        )
        hidden_all = gather_cols(hidden.astype(jnp.bfloat16))
        inner = sum_over_rows(hidden_all, inner_weight, False) + inner_bias
        active, gelu_pull = jax.vjp(exact_gelu, inner)
        active_all = gather_rows(active.astype(jnp.bfloat16))
        outer = sum_over_cols(active_all, outer_weight, False) + outer_bias
        normed_two, scale_two, result = norm_forward(hidden + outer, final_gain, final_shift)
        outcome_list.append(result.astype(jnp.bfloat16))
        grad_result = cotangent[micro_index].astype(jnp.float32)
        final_gain_part = jnp.sum(grad_result * normed_two, axis=0)
        final_shift_part = jnp.sum(grad_result, axis=0)
        grad_second = norm_backward(grad_result, normed_two, scale_two, final_gain)
        grad_outer_all = gather_cols(grad_second.astype(jnp.bfloat16))
        outer_weight_part = transpose_product(active_all, grad_outer_all)
        outer_bias_part = jnp.sum(grad_outer_all.astype(jnp.float32), axis=0)
        grad_active = sum_over_rows(grad_outer_all, outer_weight, True)
        grad_inner_all = gather_rows(gelu_pull(grad_active)[0].astype(jnp.bfloat16))
        inner_weight_part = transpose_product(hidden_all, grad_inner_all)
        inner_bias_part = jnp.sum(grad_inner_all.astype(jnp.float32), axis=0)
        grad_hidden = sum_over_cols(grad_inner_all, inner_weight, True) + grad_second
        norm_gain_part = jnp.sum(grad_hidden * normed_one, axis=0)
        norm_shift_part = jnp.sum(grad_hidden, axis=0)
        grad_first = norm_backward(grad_hidden, normed_one, scale_one, norm_gain)
        grad_branch_all = gather_cols(grad_first.astype(jnp.bfloat16))
        out_weight_part = transpose_product(attended_all, grad_branch_all)
        out_bias_part = jnp.sum(grad_branch_all.astype(jnp.float32), axis=0)
        grad_attended = sum_over_rows(grad_branch_all, out_weight, True)
        grad_mixed = grad_attended.astype(jnp.bfloat16).reshape(block_rows, heads_here, HDIM)
        grad_query, grad_keys_cat, grad_values_cat, mask_part = attend_back(
            query, keys_cat, values_cat, visible, mask_table, log_total, grad_mixed
        )
        gate_running_total = gate_running_total + fold_mask(mask_part, row_offset)
        key_full = spread_rows(grad_keys_cat, window_start, group_rows)
        value_full = spread_rows(grad_values_cat, window_start, group_rows)
        grad_keys, value_sensitivity = (
            lax.psum_scatter(
                key_full.astype(jnp.bfloat16), "row", scatter_dimension=0, tiled=True
            ).astype(jnp.float32),
            lax.psum_scatter(
                value_full.astype(jnp.bfloat16), "row", scatter_dimension=0, tiled=True
            ).astype(jnp.float32),
        )
        grad_joint = jnp.stack(
            [grad_query.reshape(block_rows, col_width), grad_keys, value_sensitivity], 1
        )
        grad_joint_all = gather_rows(
            grad_joint.astype(jnp.bfloat16).reshape(block_rows, 3 * col_width)
        )
        joint_weight_part = transpose_product(source_all, grad_joint_all)
        joint_sums = jnp.sum(grad_joint_all.astype(jnp.float32), axis=0).reshape(3, col_width)
        joint_bias_part = jnp.stack([joint_sums[0], joint_sums[2]])
        grad_list.append(sum_over_cols(grad_joint_all, joint_flat, True) + grad_first)
        weight_step = (
            joint_weight_part,
            joint_bias_part,
            out_weight_part,
            out_bias_part,
            inner_weight_part,
            inner_bias_part,
            outer_weight_part,
            outer_bias_part,
        )
        norm_step = (norm_gain_part, norm_shift_part, final_gain_part, final_shift_part)
        weight_acc = jax.tree.map(jnp.add, weight_acc, weight_step)
        norm_acc = jax.tree.map(jnp.add, norm_acc, norm_step)
    weight_acc, norm_acc = reduce_params(weight_acc, norm_acc)
    gate_backward_factor = collapse_mask_gradient(
        gate_running_total * gate_open_chance * (1.0 - gate_open_chance) / relaxation_heat
    )
    return (
        jnp.stack(outcome_list),
        jnp.stack(grad_list),
        weight_acc[0].reshape(row_width, 3, col_width),
        weight_acc[1],
        weight_acc[2],
        weight_acc[3],
        norm_acc[0],
        norm_acc[1],
        weight_acc[4],
        weight_acc[5],
        weight_acc[6],
        weight_acc[7],
        norm_acc[2],
        norm_acc[3],
        gate_backward_factor,
    )


QBLOCK = 512
PAIR = 2 * HDIM
AXES = ("dp", "row", "col")


def routes(groups):
    def place(z, core, row, col):
        return ((2 * z + core) * 2 + row) * 2 + col

    spots = [
        (z, core, row, col)
        for z in range(groups // 2)
        for core in range(2)
        for row in range(2)
        for col in range(2)
    ]

    def build(move):
        return [(place(*spot), place(*move(*spot))) for spot in spots]

    table = {
        "keep": build(lambda z, k, r, c: (z, c, r, k)),
        "turn": build(lambda z, k, r, c: (z, c, 1 - r, k)),
        "core": build(lambda z, k, r, c: (z, 1 - k, r, c)),
        "row": build(lambda z, k, r, c: (z, k, 1 - r, c)),
        "col": build(lambda z, k, r, c: (z, k, r, 1 - c)),
    }
    bit = 1
    while bit < groups // 2:
        table[bit] = build(lambda z, k, r, c, bit=bit: (z ^ bit, k, r, c))
        bit *= 2
    return table


def lane_head(shape, head):
    lane = lax.broadcasted_iota(jnp.int32, shape, len(shape) - 1)
    return (lane < HDIM) if head == 0 else (lane >= HDIM)


def dot_nt(left, right):
    return lax.dot_general(left, right, (((1,), (1,)), ((), ())), preferred_element_type=jnp.float32)


def dot_nn(left, right):
    return lax.dot_general(left, right, (((1,), (0,)), ((), ())), preferred_element_type=jnp.float32)


def dot_tn(left, right):
    return lax.dot_general(left, right, (((0,), (0,)), ((), ())), preferred_element_type=jnp.float32)


def forward_kernel(core_ref, q_ref, k_ref, v_ref, mask_ref, o_ref, lse_ref):
    core = core_ref[0]
    step = pl.program_id(1)
    prompt = core * PROMPT
    here = lax.rem(step + 2 * core, 4) * QBLOCK

    def run(starts):
        query = q_ref[...]
        outs, logs = [], []
        for head in range(2):
            q_head = jnp.where(lane_head(query.shape, head), query, jnp.zeros_like(query))
            mask = mask_ref[head].astype(jnp.float32)
            scores = [dot_nt(q_head, k_ref[pl.ds(s, QBLOCK), :]) for s in starts]
            peak = scores[0]
            for other in scores[1:]:
                peak = jnp.maximum(peak, other)
            peak = jnp.max(peak, axis=1, keepdims=True)
            total = None
            mixed = None
            for s, score in zip(starts, scores):
                expo = jnp.exp(score - peak)
                total = expo if total is None else total + expo
                low = (expo * mask).astype(jnp.bfloat16)
                part = dot_nn(low, v_ref[pl.ds(s, QBLOCK), :])
                mixed = part if mixed is None else mixed + part
            total = jnp.sum(total, axis=1, keepdims=True)
            outs.append(mixed / total)
            logs.append(jnp.broadcast_to(peak + jnp.log(total), mixed.shape))
        first = lane_head(outs[0].shape, 0)
        o_ref[...] = jnp.where(first, outs[0], outs[1]).astype(jnp.bfloat16)
        lse_ref[...] = jnp.where(first, logs[0], logs[1])

    first_key = pl.multiple_of(prompt, QBLOCK)
    second_key = pl.multiple_of(prompt + QBLOCK, QBLOCK)
    own_key = pl.multiple_of(here, QBLOCK)

    @pl.when(step < 2)
    def _():
        run([first_key, second_key])

    @pl.when(step >= 2)
    def _():
        run([first_key, second_key, own_key])


def backward_kernel(
    core_ref,
    q_ref,
    k_ref,
    v_ref,
    do_ref,
    o_ref,
    lse_ref,
    mask_ref,
    dq_ref,
    dk_ref,
    dv_ref,
    dm_ref,
    dk_acc,
    dv_acc,
):
    core = core_ref[0]
    step = pl.program_id(1)
    prompt = core * PROMPT
    here = lax.rem(step + 2 * core, 4) * QBLOCK

    @pl.when(step == 0)
    def _():
        dk_acc[...] = jnp.zeros_like(dk_acc)
        dv_acc[...] = jnp.zeros_like(dv_acc)
        dm_ref[...] = jnp.zeros_like(dm_ref)

    def run(starts):
        query = q_ref[...]
        grad = do_ref[...]
        blend = grad.astype(jnp.float32) * o_ref[...].astype(jnp.float32)
        dqs = []
        for head in range(2):
            chosen = lane_head(query.shape, head)
            q_head = jnp.where(chosen, query, jnp.zeros_like(query))
            g_head = jnp.where(chosen, grad, jnp.zeros_like(grad))
            delta = jnp.sum(jnp.where(chosen, blend, 0.0), axis=1, keepdims=True)
            log_total = lse_ref[:, head * HDIM : head * HDIM + 1]
            mask = mask_ref[head].astype(jnp.float32)
            dq = None
            for s in starts:
                rows = pl.ds(s, QBLOCK)
                prob = jnp.exp(dot_nt(q_head, k_ref[rows, :]) - log_total)
                low = (prob * mask).astype(jnp.bfloat16)
                dv_acc[rows, :] += dot_tn(low, g_head)
                pull = dot_nt(g_head, v_ref[rows, :]) * prob
                dm_ref[head] += pull
                slope = (pull * mask - prob * delta).astype(jnp.bfloat16)
                dk_acc[rows, :] += dot_tn(slope, q_head)
                part = dot_nn(slope, k_ref[rows, :])
                dq = part if dq is None else dq + part
            dqs.append(dq)
        dq_ref[...] = jnp.where(lane_head(dqs[0].shape, 0), dqs[0], dqs[1]).astype(jnp.bfloat16)

    first_key = pl.multiple_of(prompt, QBLOCK)
    second_key = pl.multiple_of(prompt + QBLOCK, QBLOCK)
    own_key = pl.multiple_of(here, QBLOCK)

    @pl.when(step < 2)
    def _():
        run([first_key, second_key])

    @pl.when(step >= 2)
    def _():
        run([first_key, second_key, own_key])

    @pl.when(step == 3)
    def _():
        dk_ref[...] = dk_acc[...].astype(jnp.bfloat16)
        dv_ref[...] = dv_acc[...].astype(jnp.bfloat16)


def attention_forward(core, joint, mask):
    rows = joint.shape[0]
    pairs = mask.shape[0] // 2
    block = lambda p, j, core_ref: (lax.rem(j + 2 * core_ref[0], 4), p)
    return pl.pallas_call(
        forward_kernel,
        grid_spec=pltpu.PrefetchScalarGridSpec(
            num_scalar_prefetch=1,
            grid=(pairs, 4),
            in_specs=[
                pl.BlockSpec((QBLOCK, PAIR), block),
                pl.BlockSpec((rows, PAIR), lambda p, j, core_ref: (0, pairs + p)),
                pl.BlockSpec((rows, PAIR), lambda p, j, core_ref: (0, 2 * pairs + p)),
                pl.BlockSpec((2, MASK_LEN, MASK_LEN), lambda p, j, core_ref: (p, 0, 0)),
            ],
            out_specs=[
                pl.BlockSpec((QBLOCK, PAIR), block),
                pl.BlockSpec((QBLOCK, PAIR), block),
            ],
        ),
        out_shape=[
            jax.ShapeDtypeStruct((rows, pairs * PAIR), jnp.bfloat16),
            jax.ShapeDtypeStruct((rows, pairs * PAIR), jnp.float32),
        ],
        compiler_params=pltpu.CompilerParams(
            dimension_semantics=("arbitrary", "arbitrary"), vmem_limit_bytes=56 * 2**20
        ),
        cost_estimate=pl.CostEstimate(
            flops=20 * pairs * 4 * 512 * 512 * 256, bytes_accessed=16 * 2**20, transcendentals=0
        ),
        name="attention_forward",
    )(core, joint, joint, joint, mask)


def attention_backward(core, joint, grad, mixed, log_total, mask):
    rows = joint.shape[0]
    pairs = mask.shape[0] // 2
    block = lambda p, j, core_ref: (lax.rem(j + 2 * core_ref[0], 4), p)
    whole = lambda p, j, core_ref: (0, p)
    tables = lambda p, j, core_ref: (p, 0, 0)
    return pl.pallas_call(
        backward_kernel,
        grid_spec=pltpu.PrefetchScalarGridSpec(
            num_scalar_prefetch=1,
            grid=(pairs, 4),
            in_specs=[
                pl.BlockSpec((QBLOCK, PAIR), block),
                pl.BlockSpec((rows, PAIR), lambda p, j, core_ref: (0, pairs + p)),
                pl.BlockSpec((rows, PAIR), lambda p, j, core_ref: (0, 2 * pairs + p)),
                pl.BlockSpec((QBLOCK, PAIR), block),
                pl.BlockSpec((QBLOCK, PAIR), block),
                pl.BlockSpec((QBLOCK, PAIR), block),
                pl.BlockSpec((2, MASK_LEN, MASK_LEN), tables),
            ],
            out_specs=[
                pl.BlockSpec((QBLOCK, PAIR), block),
                pl.BlockSpec((rows, PAIR), whole),
                pl.BlockSpec((rows, PAIR), whole),
                pl.BlockSpec((2, MASK_LEN, MASK_LEN), tables),
            ],
            scratch_shapes=[pltpu.VMEM((rows, PAIR), jnp.float32)] * 2,
        ),
        out_shape=[jax.ShapeDtypeStruct((rows, pairs * PAIR), jnp.bfloat16)] * 3
        + [jax.ShapeDtypeStruct((2 * pairs, MASK_LEN, MASK_LEN), jnp.float32)],
        compiler_params=pltpu.CompilerParams(
            dimension_semantics=("arbitrary", "arbitrary"), vmem_limit_bytes=56 * 2**20
        ),
        cost_estimate=pl.CostEstimate(
            flops=20 * pairs * 10 * 512 * 512 * 256, bytes_accessed=32 * 2**20, transcendentals=0
        ),
        name="attention_backward",
    )(core, joint, joint, joint, grad, mixed, log_total, mask)


def plus(left, right):
    return (left.astype(jnp.float32) + right.astype(jnp.float32)).astype(jnp.bfloat16)


def local_norm(values, gain, shift):
    mean = jnp.mean(values, axis=-1, keepdims=True)
    center = values - mean
    scale = lax.rsqrt(jnp.mean(center * center, axis=-1, keepdims=True) + norm_eps)
    normed = center * scale
    return (normed, scale, normed * gain + shift)


def local_norm_back(grad_out, normed, scale, gain):
    scaled = grad_out * gain
    first = jnp.mean(scaled, axis=-1, keepdims=True)
    second = jnp.mean(scaled * normed, axis=-1, keepdims=True)
    return scale * (scaled - first - normed * second)


def on_chip(
    tokens,
    joint_weight,
    joint_bias,
    out_weight,
    out_bias,
    norm_gain,
    norm_shift,
    inner_weight,
    inner_bias,
    outer_weight,
    outer_bias,
    final_gain,
    final_shift,
    trained_gate_scores,
    mask_noise,
    cotangent,
):
    low = jnp.bfloat16
    groups = lax.axis_size("dp")
    table = routes(groups)
    bits = [bit for bit in table if isinstance(bit, int)]
    row = lax.axis_index("row")
    group = lax.axis_index("dp")
    core = lax.rem(group, 2)
    height = lax.div(group, 2)
    core_word = jnp.reshape(core, (1,)).astype(jnp.int32)
    half_rows, width = tokens.shape[1:]
    heads_here = trained_gate_scores.shape[0]
    col_width = joint_weight.shape[2]
    slim = col_width // 2
    units = inner_weight.shape[1] // 2
    taken = heads_here // 2

    def send(value, way):
        return lax.ppermute(value, AXES, table[way])

    def pick(value, index, axis):
        return lax.dynamic_index_in_dim(value, index, axis, keepdims=False)

    def mine_first(value, axis):
        parts = value.reshape(value.shape[:axis] + (2, value.shape[axis] // 2) + value.shape[axis + 1 :])
        return (pick(parts, core, axis), pick(parts, 1 - core, axis))

    def in_order(mine, other, axis):
        first = jnp.where(core == 0, mine, other)
        second = jnp.where(core == 0, other, mine)
        return jnp.concatenate([first, second], axis)

    def enter(whole):
        return jnp.concatenate(
            [send(pick(whole, row, 0), "keep"), send(pick(whole, 1 - row, 0), "turn")], 1
        )

    def leave(full):
        kept = send(full[:, :width], "keep")
        turned = send(full[:, width:], "turn")
        lead = jnp.where(row == 0, kept, turned)
        trail = jnp.where(row == 0, turned, kept)
        return jnp.stack([lead, trail])

    source = enter(tokens)
    source_all = jnp.concatenate([source, send(source, "core")], 0)
    joint_parts = joint_weight.transpose(1, 0, 2)
    joint_mine = mine_first(joint_parts, 2)[0]
    joint_mine = jnp.concatenate([joint_mine[:1] * 0.125, joint_mine[1:]], 0).astype(low)
    joint_near = jnp.concatenate([joint_mine, send(joint_mine, "row")], 1)
    joint_far = send(joint_near, "col")
    joint_full = jnp.concatenate([joint_near, joint_far], 2)
    joint_flat = joint_full.transpose(1, 0, 2).reshape(2 * width, 3 * col_width)

    row_vec = jnp.stack([out_bias, norm_gain, norm_shift, outer_bias, final_gain, final_shift])
    row_vec = jnp.concatenate([row_vec, send(row_vec, "row")], 1)
    out_bias_all, gain_one, shift_one, outer_bias_all, gain_two, shift_two = (
        row_vec[i] for i in range(6)
    )
    unit_mine, unit_other = mine_first(inner_bias, 0)
    jb_mine = mine_first(joint_bias, 1)[0] * jnp.array([[0.125], [1.0]], jnp.float32)
    col_vec = jnp.concatenate([unit_mine, unit_other, jb_mine.reshape(-1)])
    col_far = send(col_vec, "col")
    inner_bias_all = jnp.concatenate(
        [unit_mine, col_far[:units], unit_other, col_far[units : 2 * units]]
    )
    jb_all = jnp.concatenate([jb_mine, col_far[2 * units :].reshape(2, slim)], 1)
    joint_bias_all = jnp.concatenate([jb_all[0], jnp.zeros_like(jb_all[0]), jb_all[1]])

    def chance(scores, noise):
        return jax.nn.sigmoid((scores + jnp.log(noise) - jnp.log1p(-noise)) / relaxation_heat)

    mask_mine = chance(
        lax.dynamic_slice_in_dim(trained_gate_scores, core * taken, taken, 0),
        lax.dynamic_slice_in_dim(mask_noise, core * taken, taken, 0),
    ).astype(low)
    mask = jnp.concatenate([mask_mine, send(mask_mine, "col")], 0)

    joint = (jnp.dot(source_all, joint_flat, preferred_element_type=jnp.float32) + joint_bias_all).astype(low)
    mixed, log_total = attention_forward(core_word, joint, mask)

    ow = mine_first(out_weight, 0)[0]
    ow = jnp.concatenate([ow, send(ow, "col")], 0)
    ow = jnp.concatenate([ow, send(ow, "row")], 1)
    out_full = jnp.concatenate([ow, send(ow, "core")], 0)
    iw = mine_first(inner_weight, 1)[0]
    iw = jnp.concatenate([iw, send(iw, "row")], 0)
    iw = jnp.concatenate([iw, send(iw, "col")], 1)
    inner_full = jnp.concatenate([iw, send(iw, "core")], 1)
    uw = mine_first(outer_weight, 0)[0]
    uw = jnp.concatenate([uw, send(uw, "col")], 0)
    uw = jnp.concatenate([uw, send(uw, "row")], 1)
    outer_full = jnp.concatenate([uw, send(uw, "core")], 0)
    grad_result = enter(cotangent).astype(jnp.float32)

    attended = jnp.concatenate([mixed[:half_rows], send(mixed[half_rows:], "core")], 1)
    branch = jnp.dot(attended, out_full, preferred_element_type=jnp.float32) + out_bias_all
    normed_one, scale_one, hidden = local_norm(
        source.astype(jnp.float32) + branch, gain_one, shift_one
    )
    hidden_low = hidden.astype(low)
    inner = jnp.dot(hidden_low, inner_full, preferred_element_type=jnp.float32) + inner_bias_all
    open_part = 0.5 + 0.5 * lax.erf(inner * 0.7071067811865476)
    active = (inner * open_part).astype(low)
    bend = (open_part + inner * jnp.exp(-0.5 * inner * inner) * 0.3989422804014327).astype(low)
    outer = jnp.dot(active, outer_full, preferred_element_type=jnp.float32) + outer_bias_all
    normed_two, scale_two, result = local_norm(hidden + outer, gain_two, shift_two)
    output = leave(result.astype(low))

    grad_second = local_norm_back(grad_result, normed_two, scale_two, gain_two)
    grad_outer = grad_second.astype(low)
    grad_active = multiply(grad_outer, outer_full, True)
    grad_inner = (grad_active * bend.astype(jnp.float32)).astype(low)
    grad_hidden = multiply(grad_inner, inner_full, True) + grad_second
    grad_first = local_norm_back(grad_hidden, normed_one, scale_one, gain_one)
    grad_branch = grad_first.astype(low)
    grad_attended = multiply(grad_branch, out_full, True).astype(low)
    grad_mixed = jnp.concatenate(
        [grad_attended[:, :col_width], send(grad_attended[:, col_width:], "core")], 0
    )

    grad_q, grad_k, grad_v, mask_part = attention_backward(
        core_word, joint, grad_mixed, mixed, log_total, mask
    )

    def over_height(value):
        for bit in bits:
            value = plus(value, send(value, bit))
        return value

    both = units * 2
    dw2_far = send(transpose_product(active[:, both:], grad_outer).astype(low), "core")
    dw2 = plus(transpose_product(active[:, :both], grad_outer), dw2_far)
    dw2 = plus(dw2[:units], send(dw2[units:], "col"))
    dw2 = plus(dw2[:, :width], send(dw2[:, width:], "row"))
    dw2 = over_height(dw2)
    grad_outer_weight = in_order(dw2, send(dw2, "core"), 0).astype(jnp.float32)

    dw1_far = send(transpose_product(hidden_low, grad_inner[:, both:]).astype(low), "core")
    dw1 = plus(transpose_product(hidden_low, grad_inner[:, :both]), dw1_far)
    dw1 = plus(dw1[:width], send(dw1[width:], "row"))
    dw1 = plus(dw1[:, :units], send(dw1[:, units:], "col"))
    dw1 = over_height(dw1)
    grad_inner_weight = in_order(dw1, send(dw1, "core"), 1).astype(jnp.float32)

    dwo_far = send(transpose_product(attended[:, col_width:], grad_branch).astype(low), "core")
    dwo = plus(transpose_product(attended[:, :col_width], grad_branch), dwo_far)
    dwo = plus(dwo[:slim], send(dwo[slim:], "col"))
    dwo = plus(dwo[:, :width], send(dwo[:, width:], "row"))
    dwo = over_height(dwo)
    grad_out_weight = in_order(dwo, send(dwo, "core"), 0).astype(jnp.float32)

    row_sums = jnp.stack(
        [
            jnp.sum(grad_branch.astype(jnp.float32), axis=0),
            jnp.sum(grad_hidden * normed_one, axis=0),
            jnp.sum(grad_hidden, axis=0),
            jnp.sum(grad_outer.astype(jnp.float32), axis=0),
            jnp.sum(grad_result * normed_two, axis=0),
            jnp.sum(grad_result, axis=0),
        ]
    )
    unit_sums = jnp.sum(grad_inner.astype(jnp.float32), axis=0).reshape(2, 2, units)
    unit_near = in_order(unit_sums[0, 0], unit_sums[1, 0], 0)
    unit_far = in_order(unit_sums[0, 1], unit_sums[1, 1], 0)
    row_sums = row_sums[:, :width] + send(row_sums[:, width:], "row")
    row_sums = row_sums + send(row_sums, "col")
    unit_sum = unit_near + send(unit_far, "col")
    unit_sum = unit_sum + send(unit_sum, "row")
    vector = jnp.concatenate([row_sums.reshape(-1), unit_sum])
    for way in ["core"] + bits:
        vector = vector + send(vector, way)
    row_grads = vector[: row_sums.size].reshape(row_sums.shape)
    grad_inner_bias = vector[row_sums.size :]

    grad_joint = jnp.concatenate([grad_q, grad_k, grad_v], 1)
    grad_source = multiply(grad_joint, joint_flat, True)
    grad_source = (
        grad_source[:half_rows]
        + send(grad_source[half_rows:].astype(low), "core").astype(jnp.float32)
        + grad_first
    )
    grad_tokens = leave(grad_source.astype(low)).astype(jnp.float32)
    dwj = transpose_product(source_all, grad_joint).astype(low).reshape(2, width, 3, 2, slim)
    dwj = plus(dwj[0], send(dwj[1], "row"))
    dwj = plus(dwj[:, :, 0], send(dwj[:, :, 1], "col"))
    dwj = over_height(dwj)
    grad_joint_weight = in_order(dwj, send(dwj, "core"), 2).astype(jnp.float32)
    grad_joint_weight = grad_joint_weight * jnp.array([0.125, 1.0, 1.0], jnp.float32)[None, :, None]
    joint_sums = jnp.sum(grad_joint.astype(jnp.float32), axis=0).reshape(3, 2, slim)
    joint_sums = jnp.stack([joint_sums[0] * 0.125, joint_sums[2]])
    joint_sums = joint_sums[:, 0] + send(joint_sums[:, 1], "col")
    for way in ["row"] + bits:
        joint_sums = joint_sums + send(joint_sums, way)
    grad_joint_bias = in_order(joint_sums, send(joint_sums, "core"), 1)

    heights = groups // 2
    strip = MASK_LEN // (2 * groups)
    pulled = mask_part[:taken] + send(mask_part[taken:].astype(low), "col").astype(jnp.float32)
    pulled = pulled.astype(low).reshape(taken, heights, 2, 2, strip, MASK_LEN)
    pulled = plus(pick(pulled, row, 3), send(pick(pulled, 1 - row, 3), "row"))
    mine = pick(pulled, core, 2)
    other = send(pick(pulled, 1 - core, 2), "core")
    pulled = in_order(mine, other, 0)
    span = heights
    level = height
    for bit in reversed(bits):
        parts = pulled.reshape(heads_here, 2, span // 2, strip, MASK_LEN)
        upper = lax.div(level, bit)
        pulled = plus(pick(parts, upper, 1), send(pick(parts, 1 - upper, 1), bit))
        level = lax.rem(level, bit)
        span = span // 2
    pulled = pulled.reshape(heads_here, strip, MASK_LEN).astype(jnp.float32)
    first_row = (group * 2 + row) * strip
    gate = chance(
        lax.dynamic_slice_in_dim(trained_gate_scores, first_row, strip, 1),
        lax.dynamic_slice_in_dim(mask_noise, first_row, strip, 1),
    )
    grad_mask = pulled * gate * (1.0 - gate) / relaxation_heat

    return (
        output,
        grad_tokens,
        grad_joint_weight,
        grad_joint_bias,
        grad_out_weight,
        row_grads[0],
        row_grads[1],
        row_grads[2],
        grad_inner_weight,
        grad_inner_bias,
        grad_outer_weight,
        row_grads[3],
        row_grads[4],
        row_grads[5],
        grad_mask,
    )


def solution(mesh):
    sizes = dict(mesh.shape)
    heights = sizes["dp"] // 2
    square = sizes["row"] == 2 and sizes["col"] == 2
    paired = sizes["dp"] % 2 == 0 and heights & (heights - 1) == 0 and MASK_LEN % (2 * sizes["dp"]) == 0
    body = on_chip if square and paired else on_device
    placed = (
        P(None, ("dp", "col"), "row"),
        P("row", None, "col"),
        P(None, "col"),
        P("col", "row"),
        P("row"),
        P("row"),
        P("row"),
        P("row", "col"),
        P("col"),
        P("col", "row"),
        P("row"),
        P("row"),
        P("row"),
        P("col", None, None),
        P("col", None, None),
        P(None, ("dp", "col"), "row"),
    )
    return jax.shard_map(
        body,
        mesh=mesh,
        in_specs=placed,
        out_specs=(
            P(None, ("dp", "col"), "row"),
            P(None, ("dp", "col"), "row"),
            P("row", None, "col"),
            P(None, "col"),
            P("col", "row"),
            P("row"),
            P("row"),
            P("row"),
            P("row", "col"),
            P("col"),
            P("col", "row"),
            P("row"),
            P("row"),
            P("row"),
            P("col", ("dp", "row"), None),
        ),
        check_vma=False,
    )
```
